32 devices in a mesh: mom: 4 (over y, core), tr: 2 (over x), tc: 4 (over z).
Axes of the slice: x: 2, y: 2, z: 4, core: 2. Of those that a mesh axis runs over, the one named last changes fastest.
Arguments:
- start_rows: float32 [256, 8, 8192], P('tr', 'mom', 'tc'), may hold values from -6 to 6
- sigma_start: float32 [256, 8, 8192], P('tr', 'mom', 'tc'), may hold values from -6 to 6
- history: float32 [8, 8192, 8192], P('mom', 'tr', 'tc'), may hold values from -0.0625 to 0.0625
- interaction: float32 [2, 256, 8, 8192], P(None, 'tr', None, 'tc'), may hold values from -1.2 to 1.2
Outputs:
- first_rows: float32 [256, 8, 8192], P('tr', 'mom', 'tc')
- last_rows: float32 [256, 8, 8192], P('tr', 'mom', 'tc')
- last_sigma: float32 [256, 8, 8192], P('tr', 'mom', 'tc')
The draws below stay inside these ranges and needn't reach their ends.
All inputs are finite; a program needn't handle non-finite values.
Results may differ from the reference program's by a relative error of at most 0.00011.
Values sent between devices are 32-bit elements; how exact they have to be, the bound alone decides.
A program may use at most 192 MiB of HBM per device.

```python
import jax
import jax.numpy as jnp
from jax import lax

NT = 8192
ROWS = 256
BLOCKS = 2
CORRECTORS = 2
KMOM = 8


def shard_levels(own_key, dims, shards, least, high):
    def one(position, parts):
        steps = jax.random.uniform(jax.random.fold_in(jax.random.fold_in(own_key, 6), position), (parts,), jnp.float32, least / len(shards), high / len(shards))
        return jnp.repeat(jnp.exp(steps), dims[position] // parts).reshape((-1,) + (1,) * (len(dims) - position - 1))

    loudness = one(*shards[0])
    for cut in shards[1:]:
        loudness = loudness * one(*cut)
    return loudness


def centred(stream_key, shape, width, limit, split=(), dtype=jnp.bfloat16):
    entries = width * jax.random.normal(stream_key, shape, jnp.float32)
    if split:
        entries = entries * shard_levels(stream_key, shape, split, -0.22, 0.18)
    return jnp.clip(entries, -limit, limit).astype(dtype)


def setup_inputs(seed: int = 0) -> dict:
    key_of = jax.random.split(jax.random.key(seed), 5)
    start_rows = centred(key_of[0], (ROWS, KMOM, NT), 1.0, 6.0, ((0, 2), (1, 4), (2, 4)), jnp.float32)
    sigma_start = centred(key_of[1], (ROWS, KMOM, NT), 1.0, 6.0, ((0, 2), (1, 4), (2, 4)), jnp.float32)
    history = centred(key_of[2], (KMOM, NT, NT), NT ** -0.5, 0.0625, ((0, 4), (1, 2), (2, 4)), jnp.float32)
    interaction = centred(key_of[3], (BLOCKS, ROWS, KMOM, NT), 0.2, 1.2, ((1, 2), (3, 4)), jnp.float32)
    return dict(start_rows=start_rows, sigma_start=sigma_start, history=history, interaction=interaction)


def convolve(weights_now, green):
    result = jnp.zeros(green.shape, jnp.float32)
    for shift_index in range(KMOM):
        result = result + weights_now[:, shift_index:shift_index + 1, :] * jnp.roll(green, shift_index, axis=1)
    return result


def reference(start_rows, sigma_start, history, interaction):
    green = start_rows
    energy = sigma_start
    results = []
    for block_index in range(BLOCKS):
        base_rows = green
        for sweep_index in range(CORRECTORS):
            green = base_rows + jnp.einsum('rkt,ktc->rkc', energy, history, precision=lax.Precision.HIGHEST)
            energy = convolve(interaction[block_index], green)
        results.append(green)
    return results[0], results[BLOCKS - 1], energy
```

```python
import functools

import jax
import jax.numpy as jnp
from jax import lax
from jax.experimental import pallas as pl
from jax.experimental.pallas import tpu as pltpu
from jax.sharding import PartitionSpec as P


CORRECTORS = 2
CHUNKS = 4


def halves(x):
    high = x.astype(jnp.bfloat16)
    low = (x - high.astype(jnp.float32)).astype(jnp.bfloat16)
    return high, low


def product_kernel(count, ties, *refs):
    rows_refs, history_ref, out_refs = refs[:count], refs[count], refs[count + 1 + ties:]
    step = pl.program_id(2)
    rows = rows_refs[0].shape[2]
    total = count * rows
    x = jnp.concatenate([ref[0, 0] for ref in rows_refs], axis=0)
    x_high, x_low = halves(x)
    h_high, h_low = halves(history_ref[0])
    both = jnp.dot(
        jnp.concatenate([x_high, x_low], axis=0), h_high, preferred_element_type=jnp.float32
    )
    value = both[:total] + both[total:] + jnp.dot(x_high, h_low, preferred_element_type=jnp.float32)

    @pl.when(step == 0)
    def _():
        for index, ref in enumerate(out_refs):
            ref[0] = value[index * rows:(index + 1) * rows]

    @pl.when(step != 0)
    def _():
        for index, ref in enumerate(out_refs):
            ref[0] += value[index * rows:(index + 1) * rows]


def tie_spec(array):
    zeros = (0,) * array.ndim
    return pl.BlockSpec((1,) * (array.ndim - 2) + (8, 128), lambda *_: zeros)


def product(parts, history, ties):
    count = len(parts)
    pieces, momenta, rows, times = parts[0].shape
    columns = history.shape[2]
    tile_t = min(times, 1024)
    tile_c = min(columns, 1024)
    inner = times // tile_t
    steps = pieces * inner
    part_spec = pl.BlockSpec(
        (1, 1, rows, tile_t), lambda m, c, t: (t // inner, m, 0, t % inner)
    )
    return pl.pallas_call(
        functools.partial(product_kernel, count, len(ties)),
        grid=(momenta, columns // tile_c, steps),
        in_specs=[part_spec] * count
        + [pl.BlockSpec((1, tile_t, tile_c), lambda m, c, t: (m, t, c))]
        + [tie_spec(tie) for tie in ties],
        out_specs=[pl.BlockSpec((1, rows, tile_c), lambda m, c, t: (m, 0, c))] * count,
        out_shape=[jax.ShapeDtypeStruct((momenta, rows, columns), jnp.float32)] * count,
        compiler_params=pltpu.CompilerParams(vmem_limit_bytes=48 * 1024 * 1024),
        cost_estimate=pl.CostEstimate(
            flops=6 * count * momenta * rows * pieces * times * columns,
            bytes_accessed=4 * history.size,
            transcendentals=0,
        ),
    )(*parts, history, *ties)


def convolve_kernel(masks, *refs):
    weights_ref, block_refs, out_ref = refs[0], refs[1:1 + len(masks)], refs[-1]
    own_group = lax.axis_index("mom")
    total_count = weights_ref.shape[0]
    local_count = out_ref.shape[0]
    for own in range(local_count):
        total = None
        for mask, ref in zip(masks, block_refs):
            other_group = own_group ^ mask
            for other in range(local_count):
                shift = (own_group - other_group) * local_count + own - other + total_count
                term = weights_ref[lax.rem(shift, total_count)] * ref[other]
                total = term if total is None else total + term
        out_ref[own] = total


def convolution(weights, masks, blocks, ties):
    momenta, rows, columns = blocks[0].shape
    total_count = weights.shape[0]
    tile = min(columns, 1024)
    spec = pl.BlockSpec((momenta, rows, tile), lambda c: (0, 0, c))
    return pl.pallas_call(
        functools.partial(convolve_kernel, masks),
        grid=(columns // tile,),
        in_specs=[pl.BlockSpec((total_count, rows, tile), lambda c: (0, 0, c))]
        + [spec] * len(blocks)
        + [tie_spec(tie) for tie in ties],
        out_specs=spec,
        out_shape=jax.ShapeDtypeStruct(blocks[0].shape, jnp.float32),
        compiler_params=pltpu.CompilerParams(vmem_limit_bytes=48 * 1024 * 1024),
        cost_estimate=pl.CostEstimate(
            flops=2 * total_count * blocks[0].size,
            bytes_accessed=4 * (weights.size + (len(blocks) + 1) * blocks[0].size),
            transcendentals=0,
        ),
    )(weights, *blocks, *ties)


def body(start_rows, sigma_start, history, interaction):
    groups = lax.axis_size("mom")
    splits = lax.axis_size("tr")
    widths = lax.axis_size("tc")
    own_split = lax.axis_index("tr")
    pieces = widths // splits
    block_total = interaction.shape[0]
    rows = start_rows.shape[0] // CHUNKS

    def ring(shift):
        return [(source, (source + shift) % splits) for source in range(splits)]

    def relayout(energy):
        every = lax.all_gather(energy, "tc", axis=0)
        sent = []
        for shift in range(1, splits):
            target = (own_split + shift) % splits
            sent.append(lax.dynamic_slice_in_dim(every, target * pieces, pieces, 0))
        parts = [lax.dynamic_slice_in_dim(every, own_split * pieces, pieces, 0)]
        for shift in range(1, splits):
            parts.append(lax.ppermute(sent[shift - 1], "tr", ring(shift)))
        return parts, sent

    def reduce_rows(partial):
        total = partial[0]
        for shift in range(1, splits):
            total = total + lax.ppermute(partial[shift], "tr", ring(-shift))
        return total

    masks = tuple(range(groups))

    def spread(green):
        blocks = [green]
        for mask in masks[1:]:
            swap = [(source, source ^ mask) for source in range(groups)]
            blocks.append(lax.ppermute(green, "mom", swap))
        return blocks

    def cut(array, chunk):
        return jnp.swapaxes(array[chunk * rows:(chunk + 1) * rows], 0, 1)

    weights = [
        [cut(interaction[block], chunk) for chunk in range(CHUNKS)] for block in range(block_total)
    ]
    energies = [None] * CHUNKS
    greens = [cut(start_rows, chunk) for chunk in range(CHUNKS)]
    bases = list(greens)
    spreads = [relayout(cut(sigma_start, chunk)) for chunk in range(CHUNKS)]
    results = [[None] * CHUNKS for _ in range(block_total)]
    steps = [
        (block, sweep, chunk)
        for block in range(block_total)
        for sweep in range(CORRECTORS)
        for chunk in range(CHUNKS)
    ]

    def finish(position, blocks, ties):
        step = steps[position]
        block, _, chunk = step
        energy = convolution(weights[block][chunk], masks, blocks, ties)
        if step[:2] == steps[-1][:2]:
            energies[chunk] = energy
        else:
            spreads[chunk] = relayout(energy)

    waiting = None
    for position, step in enumerate(steps):
        block, sweep, chunk = step
        ties = []
        if position + 1 < len(steps):
            ties += spreads[steps[position + 1][2]][1]
        if waiting is not None:
            ties.append(waiting[1][0])
        partial = product(spreads[chunk][0], history, ties)
        if waiting is not None:
            finish(*waiting, partial[:1])
        if sweep == 0:
            bases[chunk] = greens[chunk]
        green = bases[chunk] + reduce_rows(partial)
        greens[chunk] = green
        if sweep == CORRECTORS - 1:
            results[block][chunk] = green
        waiting = (position, spread(green))
    finish(*waiting, [])

    def join(chunks):
        return jnp.concatenate([jnp.swapaxes(chunk, 0, 1) for chunk in chunks], axis=0)

    return (join(results[0]), join(results[block_total - 1]), join(energies))


def solution(mesh):
    return jax.shard_map(
        body,
        mesh=mesh,
        in_specs=(
            P("tr", "mom", "tc"),
            P("tr", "mom", "tc"),
            P("mom", "tr", "tc"),
            P(None, "tr", None, "tc"),
        ),
        out_specs=(P("tr", "mom", "tc"), P("tr", "mom", "tc"), P("tr", "mom", "tc")),
        check_vma=False,
    )
```

```python
import functools

import jax
import jax.numpy as jnp
from jax import lax
from jax.experimental import pallas as pl
from jax.experimental.pallas import tpu as pltpu
from jax.sharding import PartitionSpec as P


CORRECTORS = 2
CHUNKS = 4


def halves(x):
    high = x.astype(jnp.bfloat16)
    low = (x - high.astype(jnp.float32)).astype(jnp.bfloat16)
    return high, low


def product_kernel(count, ties, *refs):
    rows_refs, history_ref, out_refs = refs[:count], refs[count], refs[count + 1 + ties:]
    step = pl.program_id(2)
    rows = rows_refs[0].shape[2]
    total = count * rows
    x = jnp.concatenate([ref[0, 0] for ref in rows_refs], axis=0)
    x_high, x_low = halves(x)
    h_high, h_low = halves(history_ref[0])
    both = jnp.dot(
        jnp.concatenate([x_high, x_low], axis=0), h_high, preferred_element_type=jnp.float32
    )
    value = both[:total] + both[total:] + jnp.dot(x_high, h_low, preferred_element_type=jnp.float32)

    @pl.when(step == 0)
    def _():
        for index, ref in enumerate(out_refs):
            ref[0] = value[index * rows:(index + 1) * rows]

    @pl.when(step != 0)
    def _():
        for index, ref in enumerate(out_refs):
            ref[0] += value[index * rows:(index + 1) * rows]


def tie_spec(array):
    zeros = (0,) * array.ndim
    return pl.BlockSpec((1,) * (array.ndim - 2) + (8, 128), lambda *_: zeros)


def product(parts, history, ties):
    count = len(parts)
    pieces, momenta, rows, times = parts[0].shape
    columns = history.shape[2]
    tile_t = min(times, 1024)
    tile_c = min(columns, 1024)
    inner = times // tile_t
    steps = pieces * inner
    part_spec = pl.BlockSpec(
        (1, 1, rows, tile_t), lambda m, c, t: (t // inner, m, 0, t % inner)
    )
    return pl.pallas_call(
        functools.partial(product_kernel, count, len(ties)),
        grid=(momenta, columns // tile_c, steps),
        in_specs=[part_spec] * count
        + [pl.BlockSpec((1, tile_t, tile_c), lambda m, c, t: (m, t, c))]
        + [tie_spec(tie) for tie in ties],
        out_specs=[pl.BlockSpec((1, rows, tile_c), lambda m, c, t: (m, 0, c))] * count,
        out_shape=[jax.ShapeDtypeStruct((momenta, rows, columns), jnp.float32)] * count,
        compiler_params=pltpu.CompilerParams(vmem_limit_bytes=48 * 1024 * 1024),
        cost_estimate=pl.CostEstimate(
            flops=6 * count * momenta * rows * pieces * times * columns,
            bytes_accessed=4 * history.size,
            transcendentals=0,
        ),
    )(*parts, history, *ties)


def convolve_kernel(masks, *refs):
    weights_ref, block_refs, out_ref = refs[0], refs[1:1 + len(masks)], refs[-1]
    own_group = lax.axis_index("mom")
    total_count = weights_ref.shape[0]
    local_count = out_ref.shape[0]
    for own in range(local_count):
        total = None
        for mask, ref in zip(masks, block_refs):
            other_group = own_group ^ mask
            for other in range(local_count):
                shift = (own_group - other_group) * local_count + own - other + total_count
                term = weights_ref[lax.rem(shift, total_count)] * ref[other]
                total = term if total is None else total + term
        out_ref[own] = total


def convolution(weights, masks, blocks, ties):
    momenta, rows, columns = blocks[0].shape
    total_count = weights.shape[0]
    tile = min(columns, 1024)
    spec = pl.BlockSpec((momenta, rows, tile), lambda c: (0, 0, c))
    return pl.pallas_call(
        functools.partial(convolve_kernel, masks),
        grid=(columns // tile,),
        in_specs=[pl.BlockSpec((total_count, rows, tile), lambda c: (0, 0, c))]
        + [spec] * len(blocks)
        + [tie_spec(tie) for tie in ties],
        out_specs=spec,
        out_shape=jax.ShapeDtypeStruct(blocks[0].shape, jnp.float32),
        compiler_params=pltpu.CompilerParams(vmem_limit_bytes=48 * 1024 * 1024),
        cost_estimate=pl.CostEstimate(
            flops=2 * total_count * blocks[0].size,
            bytes_accessed=4 * (weights.size + (len(blocks) + 1) * blocks[0].size),
            transcendentals=0,
        ),
    )(weights, *blocks, *ties)


def body(start_rows, sigma_start, history, interaction):
    groups = lax.axis_size("mom")
    splits = lax.axis_size("tr")
    widths = lax.axis_size("tc")
    own_split = lax.axis_index("tr")
    pieces = widths // splits
    block_total = interaction.shape[0]
    rows = start_rows.shape[0] // CHUNKS

    def ring(shift):
        return [(source, (source + shift) % splits) for source in range(splits)]

    def relayout(energy):
        every = lax.all_gather(energy, "tc", axis=0)
        sent = []
        for shift in range(1, splits):
            target = (own_split + shift) % splits
            sent.append(lax.dynamic_slice_in_dim(every, target * pieces, pieces, 0))
        parts = [lax.dynamic_slice_in_dim(every, own_split * pieces, pieces, 0)]
        for shift in range(1, splits):
            parts.append(lax.ppermute(sent[shift - 1], "tr", ring(shift)))
        return parts, sent

    def reduce_rows(partial):
        total = partial[0]
        for shift in range(1, splits):
            total = total + lax.ppermute(partial[shift], "tr", ring(-shift))
        return total

    masks = tuple(range(groups))

    def spread(green):
        blocks = [green]
        for mask in masks[1:]:
            swap = [(source, source ^ mask) for source in range(groups)]
            blocks.append(lax.ppermute(green, "mom", swap))
        return blocks

    def cut(array, chunk):
        return jnp.swapaxes(array[chunk * rows:(chunk + 1) * rows], 0, 1)

    weights = [
        [cut(interaction[block], chunk) for chunk in range(CHUNKS)] for block in range(block_total)
    ]
    energies = [None] * CHUNKS
    greens = [cut(start_rows, chunk) for chunk in range(CHUNKS)]
    bases = list(greens)
    spreads = [relayout(cut(sigma_start, chunk)) for chunk in range(CHUNKS)]
    results = [[None] * CHUNKS for _ in range(block_total)]
    steps = [
        (block, sweep, chunk)
        for block in range(block_total)
        for sweep in range(CORRECTORS)
        for chunk in range(CHUNKS)
    ]

    def finish(position, blocks, ties):
        step = steps[position]
        block, _, chunk = step
        energy = convolution(weights[block][chunk], masks, blocks, ties)
        if step[:2] == steps[-1][:2]:
            energies[chunk] = energy
            done.append(energy)
        else:
            spreads[chunk] = relayout(energy)

    done = []
    waiting = None
    for position, step in enumerate(steps):
        block, sweep, chunk = step
        ties = list(done[-1:])
        if position == 0:
            ties += [weight for block_weights in weights for weight in block_weights]
        if position + 1 < len(steps):
            ties += spreads[steps[position + 1][2]][1]
        if waiting is not None:
            ties.append(waiting[1][0])
        partial = product(spreads[chunk][0], history, ties)
        if waiting is not None:
            finish(*waiting, partial[:1])
        if sweep == 0:
            bases[chunk] = greens[chunk]
        green = bases[chunk] + reduce_rows(partial)
        greens[chunk] = green
        if sweep == CORRECTORS - 1:
            results[block][chunk] = green
        waiting = (position, spread(green))
    finish(*waiting, [])

    def join(chunks):
        return jnp.concatenate([jnp.swapaxes(chunk, 0, 1) for chunk in chunks], axis=0)

    return (join(results[0]), join(results[block_total - 1]), join(energies))


def solution(mesh):
    return jax.shard_map(
        body,
        mesh=mesh,
        in_specs=(
            P("tr", "mom", "tc"),
            P("tr", "mom", "tc"),
            P("mom", "tr", "tc"),
            P(None, "tr", None, "tc"),
        ),
        out_specs=(P("tr", "mom", "tc"), P("tr", "mom", "tc"), P("tr", "mom", "tc")),
        check_vma=False,
    )
```
